256 devices in a mesh: seq: 8 (over y, core), head: 32 (over x, z).
Axes of the slice: x: 4, y: 4, z: 8, core: 2. Of those that a mesh axis runs over, the one named last changes fastest.
Arguments:
- query_rows: float32 [2, 16384, 4096], P(None, 'seq', 'head'), may hold values from -0.5 to 0.5
- key_rows: float32 [2, 16384, 4096], P(None, 'seq', 'head'), may hold values from -6 to 6
- value_rows: float32 [2, 16384, 4096], P(None, 'seq', 'head'), may hold values from -6 to 6
- cotangent: float32 [2, 16384, 4096], P(None, 'seq', 'head'), may hold values from -6 to 6
- selector: int32 [2, 32, 16384], P(None, 'head', 'seq'), may hold values from 0 to 15
- level_table: float32 [16, 4], replicated, may hold values from 0.05 to 1
- span_length: int32 [2, 8], P(None, 'seq'), may hold values from 1024 to 2048
- norm_gain: float32 [4096], P('head'), may hold values from 0.1 to 1.9
Outputs:
- attended: float32 [2, 16384, 4096], P(None, 'seq', 'head')
- state_gradient: float32 [2, 8, 128, 4096], P(None, 'seq', None, 'head')
The draws below stay inside these ranges and needn't reach their ends.
Inputs may be any that keep to these rules, and one draw needn't show every extreme that they name: Keys at positions span_length and later of a block are padding.
All inputs are finite; a program needn't handle non-finite values.
Results may differ from the reference program's by a relative error of at most 0.0001.
Values sent between devices are 32-bit elements; how exact they have to be, the bound alone decides.
A program may use at most 128 MiB of HBM per device.

```python
import math
import jax
import jax.numpy as jnp
from jax import lax

DH = 128
TOK_DEV = 2048
BATCH = 2
CHOICES = 16
HEADS = 32
SEQ_BITS = 3
LEVELS = 4
TOKENS = 16384
N_SEQ = 8


def set_ends(result, own_key, low, largest):
    spot = [jax.random.randint(jax.random.fold_in(own_key, axis), (), 0, length) for axis, length in enumerate(result.shape)]
    main_axis = result.shape.index(max(result.shape))
    next_to = spot[:main_axis] + [(spot[main_axis] + 1) % result.shape[main_axis]] + spot[main_axis + 1:]
    return result.at[tuple(spot)].set(low).at[tuple(next_to)].set(largest)


def block_levels(stream_key, extent, cuts, least, largest):
    gain = 1.0
    for dim, parts in cuts:
        heights = jax.random.uniform(jax.random.fold_in(jax.random.fold_in(stream_key, 6), dim), (parts,), jnp.float32, least / len(cuts), largest / len(cuts))
        gain = gain * jnp.repeat(jnp.exp(heights), extent[dim] // parts).reshape((-1,) + (1,) * (len(extent) - 1 - dim))
    return gain


def centred(key, dims, deviation, reach, cuts=(), dtype=jnp.bfloat16):
    loudness = block_levels(key, dims, cuts, -0.22, 0.18) if cuts else 1.0
    drawn = jax.random.normal(key, dims, jnp.float32) * deviation * loudness
    return jnp.minimum(jnp.maximum(drawn, -reach), reach).astype(dtype)


def setup_inputs(seed: int = 0) -> dict:
    splits = jax.random.split(jax.random.key(seed), 9)
    query_rows = centred(splits[0], (BATCH, TOKENS, HEADS * DH), DH ** -0.5, 0.5, ((1, 8), (2, 32)), jnp.float32)
    key_rows = centred(splits[1], (BATCH, TOKENS, HEADS * DH), 1.0, 6.0, ((1, 8), (2, 32)), jnp.float32)
    value_rows = centred(splits[2], (BATCH, TOKENS, HEADS * DH), 1.0, 6.0, ((1, 8), (2, 32)), jnp.float32)
    cotangent = centred(splits[3], (BATCH, TOKENS, HEADS * DH), 1.0, 6.0, ((1, 8), (2, 32)), jnp.float32)
    selector = set_ends(jax.random.randint(splits[4], (BATCH, HEADS, TOKENS), 0, CHOICES), jax.random.fold_in(splits[4], 1), 0, CHOICES - 1).astype(jnp.int32)
    level_table = jnp.clip(jnp.exp(jax.random.uniform(splits[5], (CHOICES, LEVELS), jnp.float32, math.log(0.05), math.log(1.0))), 0.05, 1.0)
    span_length = set_ends(jax.random.randint(splits[6], (BATCH, N_SEQ), TOK_DEV // 2, TOK_DEV + 1), jax.random.fold_in(splits[6], 1), TOK_DEV // 2, TOK_DEV).astype(jnp.int32)
    norm_gain = jnp.clip(1.0 + 0.18 * jax.random.normal(splits[7], (HEADS * DH,), jnp.float32), 0.1, 1.9)
    return dict(query_rows=query_rows, key_rows=key_rows, value_rows=value_rows, cotangent=cotangent, selector=selector, level_table=level_table, span_length=span_length, norm_gain=norm_gain)


epsilon = 1e-06

def reference(query_rows, key_rows, value_rows, cotangent, selector, level_table, span_length, norm_gain):
    highest = lax.Precision.HIGHEST
    shape_five = (BATCH, N_SEQ, TOK_DEV, HEADS, DH)
    queries = query_rows.reshape(shape_five)
    values = value_rows.reshape(shape_five)
    weight = level_table[selector].reshape(BATCH, HEADS, N_SEQ, TOK_DEV, LEVELS).transpose(0, 2, 3, 1, 4)
    position = jnp.arange(TOK_DEV)
    valid = (position[None, None, :] < span_length[:, :, None]).astype(jnp.float32)
    live_keys = key_rows.reshape(shape_five) * valid[..., None, None]
    state = jnp.einsum('bjshd,bjshe->bjhde', live_keys, values, precision=highest)
    causal = position[None, :] <= position[:, None]

    def local_block(pieces):
        query_block, key_block, value_block, weight_block = pieces
        scores = jnp.einsum('thd,shd->hts', query_block, key_block, precision=highest)
        scores = jnp.where(causal[None], scores, 0.0)
        mixed = jnp.einsum('hts,she->the', scores, value_block, precision=highest)
        return mixed * weight_block[:, :, 0][:, :, None]

    def flatten(array):
        return array.reshape((BATCH * N_SEQ,) + array.shape[2:])
    local = lax.map(local_block, (flatten(queries), flatten(live_keys), flatten(values), flatten(weight)))
    combined = local.reshape(shape_five)
    device_index = jnp.arange(N_SEQ)
    members = []
    for level_bit in range(SEQ_BITS):
        reader = device_index[:, None] >> level_bit
        member = ((device_index[None, :] >> level_bit == reader ^ 1) & (reader & 1 == 1)).astype(jnp.float32)
        members.append(member)
        bucket = jnp.einsum('ij,bjhde->bihde', member, state, precision=highest)
        reads = jnp.einsum('bithd,bihde->bithe', queries, bucket, precision=highest)
        combined = combined + reads * weight[..., level_bit + 1][..., None]
    combined = combined.reshape(BATCH, TOKENS, HEADS * DH)
    full_width = HEADS * DH
    mean_square = lax.optimization_barrier(jnp.sum(combined * combined, axis=2)) / full_width
    inverse = lax.rsqrt(mean_square + epsilon)
    attended = combined * inverse[..., None] * norm_gain
    scaled = cotangent * norm_gain
    inner_sum = lax.optimization_barrier(jnp.sum(scaled * combined, axis=2))
    combined_grad = scaled * inverse[..., None] - combined * (inverse * inverse * inverse * inner_sum / full_width)[..., None]
    grad_five = combined_grad.reshape(shape_five)
    state_grad = jnp.zeros((BATCH, N_SEQ, HEADS, DH, DH), jnp.float32)
    for level_bit in range(SEQ_BITS):
        level_grad = jnp.einsum('bithd,bithe->bihde', queries * weight[..., level_bit + 1][..., None], grad_five, precision=highest)
        state_grad = state_grad + jnp.einsum('ij,bihde->bjhde', members[level_bit], level_grad, precision=highest)
    state_gradient = state_grad.transpose(0, 1, 3, 2, 4).reshape(BATCH, N_SEQ, DH, HEADS * DH)
    return (attended, state_gradient)
```

```python
import functools

import jax
import jax.numpy as jnp
from jax import lax
from jax.experimental import pallas as pl
from jax.experimental.pallas import tpu as pltpu
from jax.sharding import PartitionSpec as P

DH = 128
CHUNK = 256
WIDE = 512
EPS = 1e-06
F32 = jnp.float32
BF16 = jnp.bfloat16


def split(x):
    high = x.astype(BF16)
    return high, (x - high.astype(F32)).astype(BF16)


def mm(a, b):
    return jnp.dot(a, b, preferred_element_type=F32)


def mm_nt(a, b):
    return lax.dot_general(a, b, (((1,), (1,)), ((), ())), preferred_element_type=F32)


def remote(src, dst, send_sem, recv_sem, device):
    return pltpu.make_async_remote_copy(
        src_ref=src,
        dst_ref=dst,
        send_sem=send_sem,
        recv_sem=recv_sem,
        device_id=device,
        device_id_type=pl.DeviceIdType.MESH,
    )


def kernel(
    n_head, tokens,
    q_hbm, k_hbm, v_hbm, c_hbm, sel_ref, tab_ref, span_ref, gain_ref,
    att_hbm, sg_ref,
    qb, kb, vb, cb, kh, kl, vt, pp, wrow, wq, comb, sc, gacc, attb,
    st, b0, pair, b12, quad, lb, sums, sums_in, coef, gr, t1, t1c, r12, r12_in, r3, total, t4,
    load_sem, out_sem, send_sem, recv_sem, h_send, h_recv,
):
    n_chunks = tokens // CHUNK
    per_batch = n_head // 2
    seq = lax.axis_index("seq")
    head = lax.axis_index("head")
    core = lax.rem(seq, 2)
    other = 1 - core
    chip = lax.div(seq, 2)
    y_a = chip + 1 - 2 * lax.rem(chip, 2)
    y_b = 3 - chip
    mate = seq + 1 - 2 * core
    near = 2 * y_a + core
    far = 2 * y_b + core

    loads = {}
    for b in range(2):
        for i, (name, src, dst) in enumerate((("k", k_hbm, kb), ("v", v_hbm, vb))):
            loads[name, b] = pltpu.make_async_copy(src.at[b], dst.at[b], load_sem.at[i, b])
            loads[name, b].start()
    for b in range(2):
        for i, (name, src, dst) in enumerate((("q", q_hbm, qb), ("c", c_hbm, cb))):
            loads[name, b] = pltpu.make_async_copy(src.at[b], dst.at[b], load_sem.at[2 + i, b])
            loads[name, b].start()

    barrier = pltpu.get_barrier_semaphore()
    for peer in (mate, near, far):
        pl.semaphore_signal(barrier, 1, device_id={"seq": peer, "head": head}, device_id_type=pl.DeviceIdType.MESH)

    @pl.loop(1, n_head)
    def _(r):
        peer = lax.rem(head + r, n_head)
        pl.semaphore_signal(barrier, 1, device_id={"seq": seq, "head": peer}, device_id_type=pl.DeviceIdType.MESH)

    selector = [sel_ref[b] for b in range(2)]
    for level in range(4):
        on = 1 if level == 0 else lax.rem(lax.div(seq, 2 ** (level - 1)), 2)
        for b in range(2):
            row = jnp.zeros((1, tokens), F32)
            for choice in range(16):
                row = jnp.where(selector[b] == choice, tab_ref[choice, level], row)
            if level > 0:
                row = jnp.where(on == 1, row, 0.0)
            wrow[level * 2 + b] = row

    for b in range(2):
        loads["k", b].wait()
        loads["v", b].wait()
        span = span_ref[b, 0]

        def state_step(n, acc, b=b, span=span):
            rows = pl.ds(pl.multiple_of(n * CHUNK, CHUNK), CHUNK)
            position = n * CHUNK + lax.broadcasted_iota(jnp.int32, (CHUNK, DH), 0)
            k_hi, k_lo = split(jnp.where(position < span, kb[b, rows, :], 0.0))
            kh[b, rows, :] = k_hi
            kl[b, rows, :] = k_lo
            v_hi, v_lo = split(vb[b, rows, :].T)
            v_two = jnp.concatenate([v_hi, v_lo], axis=0)
            vt[b, n] = v_two
            p_hi, p_lo = split(acc)
            pp[b, n] = jnp.concatenate([p_hi, p_lo], axis=0)
            out = mm(v_two, jnp.concatenate([k_hi, k_lo], axis=1))
            return acc + (out[:DH, :DH] + (out[:DH, DH:] + out[DH:, :DH]))

        st[b] = lax.fori_loop(0, n_chunks, state_step, jnp.zeros((DH, DH), F32))

    pl.semaphore_wait(barrier, n_head - 1 + 3)

    def to(peer):
        return {"seq": peer, "head": head}

    s1 = remote(st, b0, send_sem.at[0], recv_sem.at[0], to(mate))
    s1.start()

    def local_chunk(b, n):
        rows = pl.ds(pl.multiple_of(n * CHUNK, CHUNK), CHUNK)
        q_t = qb[b, rows, :].T
        q_hi, q_lo = split(q_t)
        k_hi, k_lo = kh[b, rows, :], kl[b, rows, :]
        scores = mm(
            jnp.concatenate([k_hi, k_hi, k_lo], axis=1), jnp.concatenate([q_hi, q_lo, q_hi], axis=0)
        )
        key_at = lax.broadcasted_iota(jnp.int32, (CHUNK, CHUNK), 0)
        query_at = lax.broadcasted_iota(jnp.int32, (CHUNK, CHUNK), 1)
        s_hi, s_lo = split(jnp.where(key_at <= query_at, scores, 0.0))
        v_two, p_two = vt[b, n], pp[b, n]
        out = mm(
            jnp.concatenate([v_two, v_two, p_two, p_two], axis=1),
            jnp.concatenate([s_hi, s_lo, q_hi, q_lo], axis=0),
        )
        comb[b, n] = (out[:DH] + out[DH:]) * wrow[b, :, rows]
        for level in range(3):
            w_hi, w_lo = split(q_t * wrow[2 * (level + 1) + b, :, rows])
            wq[b, level * DH : (level + 1) * DH, rows] = w_hi
            wq[b, (3 + level) * DH : (4 + level) * DH, rows] = w_lo
        sc[b, n] = (cb[b, rows, :] * gain_ref[...]).T

    def local_chunks(b, low, high):
        @pl.loop(low, high)
        def _(n):
            local_chunk(b, n)

    half = n_chunks // 2
    loads["q", 0].wait()
    loads["c", 0].wait()
    local_chunks(0, 0, half)

    s1.wait_recv()
    pair[...] = st[core] + b0[core]
    s2 = remote(pair, b12.at[core, 0], send_sem.at[1], recv_sem.at[1], to(near))
    s2.start()
    local_chunks(0, half, n_chunks)
    s2.wait_recv()
    quad[...] = pair[...] + b12[core, 0]
    s3 = remote(quad, b12.at[core, 1], send_sem.at[2], recv_sem.at[2], to(far))
    s3.start()
    s4a = remote(b12.at[core, 0], b12.at[core, 0], send_sem.at[3], recv_sem.at[3], to(mate))
    s4a.start()
    loads["q", 1].wait()
    loads["c", 1].wait()
    local_chunks(1, 0, half)
    s3.wait_recv()
    s4b = remote(b12.at[core, 1], b12.at[core, 1], send_sem.at[4], recv_sem.at[4], to(mate))
    s4b.start()
    local_chunks(1, half, n_chunks)

    def head_copy(peer):
        return remote(
            sums.at[peer], sums_in.at[head], h_send.at[0], h_recv.at[0], {"seq": seq, "head": peer}
        )

    def reads(b):
        halves = [split(b0[b]), split(b12[b, 0]), split(b12[b, 1])]
        high = jnp.concatenate([h[0] for h in halves], axis=1)
        low = jnp.concatenate([h[1] for h in halves], axis=1)
        lb[b, :DH] = jnp.concatenate([high, high], axis=1)
        lb[b, DH:] = jnp.concatenate([low, low], axis=1)

        @pl.loop(0, n_chunks)
        def _(n):
            rows = pl.ds(pl.multiple_of(n * CHUNK, CHUNK), CHUNK)
            out = mm(lb[b], wq[b, :, rows])
            mixed = comb[b, n] + (out[:DH] + out[DH:])
            comb[b, n] = mixed
            square = jnp.sum(mixed * mixed, axis=0, keepdims=True)
            inner = jnp.sum(sc[b, n] * mixed, axis=0, keepdims=True)
            for part in range(2):
                owner = b * per_batch + 2 * n + part
                lanes = slice(part * DH, (part + 1) * DH)
                sums[owner, 0:1, :] = square[:, lanes]
                sums[owner, 1:2, :] = inner[:, lanes]

        @pl.loop(0, per_batch)
        def _(j):
            peer = b * per_batch + j

            @pl.when(peer != head)
            def _():
                head_copy(peer).start()

    reads(core)
    s4a.wait_recv()
    s4b.wait_recv()
    reads(other)

    def all_but_one(buffer, sem):
        window = buffer.at[pl.ds(0, n_head - 1)]
        pltpu.make_async_copy(window, window, sem).wait()

    sums_in[head] = sums[head]
    all_but_one(sums_in, h_recv.at[0])
    whole = jnp.sum(sums_in[...], axis=0)
    inverse = lax.rsqrt(whole[0:1] / (n_head * DH) + EPS)
    coef[head, 0:1, :] = inverse
    coef[head, 1:2, :] = inverse * inverse * inverse * whole[1:2] / (n_head * DH)

    @pl.loop(1, n_head)
    def _(r):
        peer = lax.rem(head + r, n_head)
        remote(
            coef.at[head], coef.at[head], h_send.at[1], h_recv.at[1], {"seq": seq, "head": peer}
        ).start()

    all_but_one(coef, h_recv.at[1])

    wide_chunks = tokens // WIDE

    def row_of(b, n, which, width):
        first = b * per_batch + n * (width // DH)
        return jnp.concatenate(
            [coef[first + i, which : which + 1, :] for i in range(width // DH)], axis=1
        )

    def level_grads(b):
        gacc[...] = jnp.zeros_like(gacc)

        @pl.loop(0, wide_chunks)
        def _(n):
            rows = pl.ds(pl.multiple_of(n * WIDE, WIDE), WIDE)
            pieces = WIDE // CHUNK
            scaled = jnp.concatenate([sc[b, n * pieces + i] for i in range(pieces)], axis=1)
            mixed = jnp.concatenate([comb[b, n * pieces + i] for i in range(pieces)], axis=1)
            grad = scaled * row_of(b, n, 0, WIDE) - mixed * row_of(b, n, 1, WIDE)
            g_hi, g_lo = split(grad)
            gacc[...] += mm_nt(wq[b, :, rows], jnp.concatenate([g_hi, g_lo], axis=0))

        for level in range(3):
            top = slice(level * DH, (level + 1) * DH)
            bottom = slice((3 + level) * DH, (4 + level) * DH)
            gr[b, level] = gacc[top, :DH] + (gacc[top, DH:] + gacc[bottom, :DH])

    def attended(b):
        @pl.loop(0, n_chunks)
        def _(n):
            rows = pl.ds(pl.multiple_of(n * CHUNK, CHUNK), CHUNK)
            attb[b, rows, :] = (comb[b, n] * row_of(b, n, 0, CHUNK)).T * gain_ref[...]

        pltpu.make_async_copy(attb.at[b], att_hbm.at[b], out_sem.at[b]).start()

    level_grads(core)
    g1 = remote(gr.at[core], t1, send_sem.at[5], recv_sem.at[5], to(mate))
    g1.start()
    level_grads(other)
    g1c = remote(gr.at[other, 0], t1c, send_sem.at[6], recv_sem.at[6], to(mate))
    g1c.start()
    g1.wait_recv()
    r12[0] = gr[other, 1] + t1[1]
    r12[1] = gr[other, 2] + t1[2]
    g2a = remote(r12.at[0], r12_in.at[0], send_sem.at[7], recv_sem.at[7], to(near))
    g2b = remote(r12.at[1], r12_in.at[1], send_sem.at[8], recv_sem.at[8], to(far))
    g2b.start()
    g2a.start()
    attended(0)
    g2b.wait_recv()
    g3 = remote(r12_in.at[1], r3, send_sem.at[9], recv_sem.at[9], to(near))
    g3.start()
    attended(1)
    g2a.wait_recv()
    g3.wait_recv()
    total[...] = r12_in[0] + r12_in[1] + r3[...]
    g4 = remote(total, t4, send_sem.at[10], recv_sem.at[10], to(mate))
    g4.start()
    sg_ref[other, 0] = total[...] + t1[0]
    g1c.wait_recv()
    g4.wait_recv()
    sg_ref[core, 0] = t4[...] + t1c[...]

    for copy in (s1, s2, s3, s4a, s4b, g1, g1c, g2a, g2b, g3, g4):
        copy.wait_send()
    all_but_one(sums, h_send.at[0])
    all_but_one(coef, h_send.at[1])
    for b in range(2):
        pltpu.make_async_copy(attb.at[b], att_hbm.at[b], out_sem.at[b]).wait()


def solution(mesh):
    n_head = mesh.shape["head"]

    def local(
        query_rows, key_rows, value_rows, cotangent, selector, level_table, span_length, norm_gain
    ):
        batch, tokens, _ = query_rows.shape
        n_chunks = tokens // CHUNK
        square = (DH, DH)
        whole = (batch, tokens, DH)
        scratch = [pltpu.VMEM(whole, F32) for _ in range(4)]
        scratch += [
            pltpu.VMEM(whole, BF16),
            pltpu.VMEM(whole, BF16),
            pltpu.VMEM((batch, n_chunks, 2 * DH, CHUNK), BF16),
            pltpu.VMEM((batch, n_chunks, 2 * DH, DH), BF16),
            pltpu.VMEM((4 * batch, 1, tokens), F32),
            pltpu.VMEM((batch, 6 * DH, tokens), BF16),
            pltpu.VMEM((batch, n_chunks, DH, CHUNK), F32),
            pltpu.VMEM((batch, n_chunks, DH, CHUNK), F32),
            pltpu.VMEM((6 * DH, 2 * DH), F32),
            pltpu.VMEM(whole, F32),
            pltpu.VMEM((batch, *square), F32),
            pltpu.VMEM((batch, *square), F32),
            pltpu.VMEM(square, F32),
            pltpu.VMEM((batch, 2, *square), F32),
            pltpu.VMEM(square, F32),
            pltpu.VMEM((batch, 2 * DH, 6 * DH), BF16),
            pltpu.VMEM((n_head, 2, DH), F32),
            pltpu.VMEM((n_head, 2, DH), F32),
            pltpu.VMEM((n_head, 2, DH), F32),
            pltpu.VMEM((batch, 3, *square), F32),
            pltpu.VMEM((3, *square), F32),
            pltpu.VMEM(square, F32),
            pltpu.VMEM((2, *square), F32),
            pltpu.VMEM((2, *square), F32),
            pltpu.VMEM(square, F32),
            pltpu.VMEM(square, F32),
            pltpu.VMEM(square, F32),
            pltpu.SemaphoreType.DMA((4, 2)),
            pltpu.SemaphoreType.DMA((2,)),
            pltpu.SemaphoreType.DMA((11,)),
            pltpu.SemaphoreType.DMA((11,)),
            pltpu.SemaphoreType.DMA((2,)),
            pltpu.SemaphoreType.DMA((2,)),
        ]
        hbm = pl.BlockSpec(memory_space=pl.ANY)
        vmem = pl.BlockSpec(memory_space=pltpu.VMEM)
        smem = pl.BlockSpec(memory_space=pltpu.SMEM)
        return pl.pallas_call(
            functools.partial(kernel, n_head, tokens),
            out_shape=(
                jax.ShapeDtypeStruct(whole, F32),
                jax.ShapeDtypeStruct((batch, 1, DH, DH), F32),
            ),
            in_specs=[hbm, hbm, hbm, hbm, vmem, smem, smem, vmem],
            out_specs=(hbm, vmem),
            scratch_shapes=scratch,
            compiler_params=pltpu.CompilerParams(
                collective_id=0, has_side_effects=True, vmem_limit_bytes=50 * 2**20
            ),
            cost_estimate=pl.CostEstimate(
                flops=2 * 10**10, bytes_accessed=12 * 2**20, transcendentals=0
            ),
        )(
            query_rows, key_rows, value_rows, cotangent, selector, level_table, span_length,
            norm_gain.reshape(1, DH),
        )

    return jax.shard_map(
        local,
        mesh=mesh,
        in_specs=(
            P(None, "seq", "head"),
            P(None, "seq", "head"),
            P(None, "seq", "head"),
            P(None, "seq", "head"),
            P(None, "head", "seq"),
            P(),
            P(None, "seq"),
            P("head"),
        ),
        out_specs=(P(None, "seq", "head"), P(None, "seq", None, "head")),
        check_vma=False,
    )
```

```python
import functools

import jax
import jax.numpy as jnp
from jax import lax
from jax.experimental import pallas as pl
from jax.experimental.pallas import tpu as pltpu
from jax.sharding import PartitionSpec as P

DH = 128
CHUNK = 256
WIDE = 2048
U_STATE = 8
U_LOCAL = 4
U_READ = 8
U_ATT = 8
N_X = 4
EPS = 1e-06
F32 = jnp.float32
BF16 = jnp.bfloat16


def split(x):
    high = x.astype(BF16)
    return high, (x - high.astype(F32)).astype(BF16)


def mm(a, b):
    return jnp.dot(a, b, preferred_element_type=F32)


def mm_nt(a, b):
    return lax.dot_general(a, b, (((1,), (1,)), ((), ())), preferred_element_type=F32)


def remote(src, dst, send_sem, recv_sem, device):
    return pltpu.make_async_remote_copy(
        src_ref=src,
        dst_ref=dst,
        send_sem=send_sem,
        recv_sem=recv_sem,
        device_id=device,
        device_id_type=pl.DeviceIdType.MESH,
    )


def kernel(
    n_x, n_z, tokens,
    q_hbm, k_hbm, v_hbm, c_hbm, sel_hbm, tab_hbm, span_hbm, gain_hbm,
    att_ref, sg_ref,
    sel_ref, tab_ref, span_ref, gain_ref,
    qb, kb, vb, cb, kh, kl, vt, pp, wrow, wq, comb, sc, gacc,
    st, b0, pair, b12, far_in, lb, x_in, z_in, coef, gr0, grh, t0, t1, r12, r_in, total,
    load_sem, small_sem, send_sem, recv_sem, h_send, h_recv,
):
    n_chunks = tokens // CHUNK
    half = DH // 2
    seq = lax.axis_index("seq")
    head = lax.axis_index("head")
    core = lax.rem(seq, 2)
    other = 1 - core
    chip = lax.div(seq, 2)
    mate = seq + 1 - 2 * core
    near = 2 * (chip + 1 - 2 * lax.rem(chip, 2)) + core
    far = 2 * (3 - chip) + core
    across = lax.rem(seq + 4, 8)
    x = lax.div(head, n_z)
    z = lax.rem(head, n_z)
    x_peers = [n_z * lax.rem(x + r, n_x) + z for r in range(1, n_x)]
    z_peers = [n_z * x + lax.rem(z + r, n_z) for r in range(1, n_z)]

    def to(peer):
        return {"seq": peer, "head": head}

    def along(peer):
        return {"seq": seq, "head": peer}

    peers = [to(p) for p in (mate, near, far, across)] + [along(p) for p in x_peers + z_peers]

    small = [
        pltpu.make_async_copy(src, dst, small_sem.at[i])
        for i, (src, dst) in enumerate(
            ((tab_hbm, tab_ref), (span_hbm, span_ref), (sel_hbm, sel_ref), (gain_hbm, gain_ref))
        )
    ]
    for copy in small:
        copy.start()
    loads = {}
    pairs = (("k", k_hbm, kb), ("v", v_hbm, vb), ("q", q_hbm, qb), ("c", c_hbm, cb))
    for first in (0, 2):
        for b in range(2):
            for i in (first, first + 1):
                name, src, dst = pairs[i]
                loads[name, b] = pltpu.make_async_copy(src.at[b], dst.at[b], load_sem.at[i, b])
                loads[name, b].start()

    barrier = pltpu.get_barrier_semaphore()
    for peer in peers:
        pl.semaphore_signal(barrier, 1, device_id=peer, device_id_type=pl.DeviceIdType.MESH)

    for copy in small:
        copy.wait()
    selector = [sel_ref[b] for b in range(2)]
    for level in range(4):
        on = 1 if level == 0 else lax.rem(lax.div(seq, 2 ** (level - 1)), 2)
        for b in range(2):
            row = jnp.zeros((1, tokens), F32)
            for choice in range(16):
                row = jnp.where(selector[b] == choice, tab_ref[level, choice], row)
            if level > 0:
                row = jnp.where(on == 1, row, 0.0)
            wrow[level * 2 + b] = row

    def lanes(n):
        return pl.ds(pl.multiple_of(n * CHUNK, CHUNK), CHUNK)

    def states(b):
        span = span_ref[0, b]

        def step(i, acc):
            for u in range(U_STATE):
                n = i * U_STATE + u
                rows = lanes(n)
                position = n * CHUNK + lax.broadcasted_iota(jnp.int32, (CHUNK, DH), 0)
                k_hi, k_lo = split(jnp.where(position < span, kb[b, rows, :], 0.0))
                kh[b, rows, :] = k_hi
                kl[b, rows, :] = k_lo
                v_hi, v_lo = split(vb[b, rows, :].T)
                v_two = jnp.concatenate([v_hi, v_lo], axis=0)
                vt[b, n] = v_two
                p_hi, p_lo = split(acc)
                pp[b, n] = jnp.concatenate([p_hi, p_lo], axis=0)
                out = mm(v_two, jnp.concatenate([k_hi, k_lo], axis=1))
                acc = acc + (out[:DH, :DH] + (out[:DH, DH:] + out[DH:, :DH]))
            return acc

        st[b] = lax.fori_loop(0, n_chunks // U_STATE, step, jnp.zeros((DH, DH), F32))

    def local_chunk(b, n):
        rows = lanes(n)
        q_t = qb[b, rows, :].T
        q_hi, q_lo = split(q_t)
        k_hi, k_lo = kh[b, rows, :], kl[b, rows, :]
        scores = mm(
            jnp.concatenate([k_hi, k_hi, k_lo], axis=1), jnp.concatenate([q_hi, q_lo, q_hi], axis=0)
        )
        key_at = lax.broadcasted_iota(jnp.int32, (CHUNK, CHUNK), 0)
        query_at = lax.broadcasted_iota(jnp.int32, (CHUNK, CHUNK), 1)
        s_hi, s_lo = split(jnp.where(key_at <= query_at, scores, 0.0))
        v_two, p_two = vt[b, n], pp[b, n]
        out = mm(
            jnp.concatenate([v_two, v_two, p_two, p_two], axis=1),
            jnp.concatenate([s_hi, s_lo, q_hi, q_lo], axis=0),
        )
        comb[b, n] = (out[:DH] + out[DH:]) * wrow[b, :, rows]
        for level in range(3):
            w_hi, w_lo = split(q_t * wrow[2 * (level + 1) + b, :, rows])
            wq[b, level * DH : (level + 1) * DH, rows] = w_hi
            wq[b, (3 + level) * DH : (4 + level) * DH, rows] = w_lo
        sc[b, n] = (cb[b, rows, :] * gain_ref[...]).T

    def local_chunks(b, low, high):
        @pl.loop(0, (high - low) // U_LOCAL)
        def _(i):
            for u in range(U_LOCAL):
                local_chunk(b, low + i * U_LOCAL + u)

    for b in range(2):
        loads["k", b].wait()
        loads["v", b].wait()
        states(b)

    pl.semaphore_wait(barrier, len(peers))

    s1, s2, s4 = {}, {}, {}
    for b in range(2):
        s1[b] = remote(st.at[b], b0.at[b], send_sem.at[0, b], recv_sem.at[0, b], to(mate))
        s1[b].start()

    def sum_pair(b):
        s1[b].wait_recv()
        mine = pl.ds(pl.multiple_of(core * half, half), half)
        pair[b] = st[b, mine, :] + b0[b, mine, :]
        s2[b] = [
            remote(pair.at[b], far_in.at[b, 0], send_sem.at[1, b], recv_sem.at[1, b], to(across)),
            remote(pair.at[b], far_in.at[b, 1], send_sem.at[2, b], recv_sem.at[2, b], to(far)),
            remote(pair.at[b], b12.at[b, core, 0], send_sem.at[3, b], recv_sem.at[3, b], to(near)),
        ]
        for copy in s2[b]:
            copy.start()

    def sum_quad(b):
        for copy in s2[b]:
            copy.wait_recv()
        b12[b, core, 1] = far_in[b, 0] + far_in[b, 1]
        s4[b] = remote(
            b12.at[b, core], b12.at[b, core], send_sem.at[4, b], recv_sem.at[4, b], to(mate)
        )
        s4[b].start()

    middle = n_chunks // 2
    loads["q", 0].wait()
    loads["c", 0].wait()
    local_chunks(0, 0, middle)
    sum_pair(0)
    sum_pair(1)
    local_chunks(0, middle, n_chunks)
    loads["q", 1].wait()
    loads["c", 1].wait()
    local_chunks(1, 0, middle)
    sum_quad(0)
    sum_quad(1)
    local_chunks(1, middle, n_chunks)

    def reads(b):
        halves = [split(b0[b])]
        for level in range(2):
            halves.append(split(jnp.concatenate([b12[b, 0, level], b12[b, 1, level]], axis=0)))
        high = jnp.concatenate([h[0] for h in halves], axis=1)
        low = jnp.concatenate([h[1] for h in halves], axis=1)
        lb[b, :DH] = jnp.concatenate([high, high], axis=1)
        lb[b, DH:] = jnp.concatenate([low, low], axis=1)

        @pl.loop(0, n_chunks // U_READ)
        def _(i):
            for u in range(U_READ):
                n = i * U_READ + u
                out = mm(lb[b], wq[b, :, lanes(n)])
                mixed = comb[b, n] + (out[:DH] + out[DH:])
                comb[b, n] = mixed
                x_in[b, x, pl.ds(n, 1), :] = jnp.sum(mixed * mixed, axis=0, keepdims=True)
                x_in[b, x, pl.ds(n_chunks + n, 1), :] = jnp.sum(
                    sc[b, n] * mixed, axis=0, keepdims=True
                )

    def send_x(b):
        for peer in reversed(x_peers):
            remote(x_in.at[b, x], x_in.at[b, x], h_send.at[0, b], h_recv.at[0, b], along(peer)).start()

    def arrived(buffer, count, sem):
        window = buffer.at[pl.ds(0, count)]
        pltpu.make_async_copy(window, window, sem).wait()

    def send_z(b):
        arrived(x_in.at[b], n_x - 1, h_recv.at[0, b])
        z_in[b, z] = jnp.sum(x_in[b], axis=0)
        for peer in sorted(range(1, n_z), key=lambda r: -min(r, n_z - r)):
            remote(
                z_in.at[b, z], z_in.at[b, z], h_send.at[1, b], h_recv.at[1, b],
                along(z_peers[peer - 1]),
            ).start()

    def coefficients(b):
        arrived(z_in.at[b], n_z - 1, h_recv.at[1, b])
        whole = jnp.sum(z_in[b], axis=0)
        width = n_x * n_z * DH
        inverse = lax.rsqrt(whole[:n_chunks] / width + EPS)
        coef[b, :n_chunks] = inverse
        coef[b, n_chunks:] = inverse * inverse * inverse * whole[n_chunks:] / width

    for b in range(2):
        s4[b].wait_recv()
        reads(b)
        send_x(b)
    for b in range(2):
        send_z(b)

    def level_grads(b):
        gacc[...] = jnp.zeros_like(gacc)
        pieces = WIDE // CHUNK

        @pl.loop(0, tokens // WIDE)
        def _(n):
            parts = []
            for i in range(pieces):
                m = n * pieces + i
                grad = sc[b, m] * coef[b, pl.ds(m, 1), :] - comb[b, m] * coef[b, pl.ds(n_chunks + m, 1), :]
                parts.append(jnp.concatenate(split(grad), axis=0))
            rows = pl.ds(pl.multiple_of(n * WIDE, WIDE), WIDE)
            gacc[...] += mm_nt(wq[b, :, rows], jnp.concatenate(parts, axis=1))

        for level in range(3):
            top = slice(level * DH, (level + 1) * DH)
            bottom = slice((3 + level) * DH, (4 + level) * DH)
            grad = gacc[top, :DH] + (gacc[top, DH:] + gacc[bottom, :DH])
            if level == 0:
                gr0[b] = grad
            else:
                grh[b, 0, level - 1] = grad[:half]
                grh[b, 1, level - 1] = grad[half:]

    def attended(b):
        @pl.loop(0, n_chunks // U_ATT)
        def _(i):
            for u in range(U_ATT):
                n = i * U_ATT + u
                att_ref[b, lanes(n), :] = (comb[b, n] * coef[b, pl.ds(n, 1), :]).T * gain_ref[...]

    g1, g2, g4 = {}, {}, {}

    def send_mate(b):
        g1[b] = [
            remote(grh.at[b, other], t1.at[b], send_sem.at[5, b], recv_sem.at[5, b], to(mate)),
            remote(gr0.at[b], t0.at[b], send_sem.at[6, b], recv_sem.at[6, b], to(mate)),
        ]
        for copy in g1[b]:
            copy.start()

    def send_chips(b):
        g1[b][0].wait_recv()
        r12[b] = grh[b, core] + t1[b]
        g2[b] = [
            remote(r12.at[b, 1], r_in.at[b, 0], send_sem.at[7, b], recv_sem.at[7, b], to(across)),
            remote(r12.at[b, 1], r_in.at[b, 1], send_sem.at[8, b], recv_sem.at[8, b], to(far)),
            remote(r12.at[b, 0], r_in.at[b, 2], send_sem.at[9, b], recv_sem.at[9, b], to(near)),
        ]
        for copy in g2[b]:
            copy.start()

    def send_total(b):
        for copy in g2[b]:
            copy.wait_recv()
        total[b, core] = r_in[b, 0] + r_in[b, 1] + r_in[b, 2]
        g4[b] = remote(
            total.at[b, core], total.at[b, core], send_sem.at[10, b], recv_sem.at[10, b], to(mate)
        )
        g4[b].start()

    for b in range(2):
        coefficients(b)
        level_grads(b)
        send_mate(b)
    send_chips(0)
    send_chips(1)
    attended(0)
    attended(1)
    send_total(0)
    send_total(1)
    for b in range(2):
        g1[b][1].wait_recv()
        g4[b].wait_recv()
        sg_ref[b, 0, :half] = total[b, 0] + t0[b, :half]
        sg_ref[b, 0, half:] = total[b, 1] + t0[b, half:]

    for b in range(2):
        for copy in (s1[b], s4[b], g4[b], *s2[b], *g1[b], *g2[b]):
            copy.wait_send()
        arrived(x_in.at[b], n_x - 1, h_send.at[0, b])
        arrived(z_in.at[b], n_z - 1, h_send.at[1, b])


def solution(mesh):
    n_z = mesh.shape["head"] // N_X

    def local(
        query_rows, key_rows, value_rows, cotangent, selector, level_table, span_length, norm_gain
    ):
        batch, tokens, _ = query_rows.shape
        n_chunks = tokens // CHUNK
        square = (DH, DH)
        half = (DH // 2, DH)
        whole = (batch, tokens, DH)
        scratch = [
            pltpu.VMEM((batch, 1, tokens), jnp.int32),
            pltpu.SMEM((4, 16), F32),
            pltpu.SMEM((1, batch), jnp.int32),
            pltpu.VMEM((1, DH), F32),
        ]
        scratch += [pltpu.VMEM(whole, F32) for _ in range(4)]
        scratch += [
            pltpu.VMEM(whole, BF16),
            pltpu.VMEM(whole, BF16),
            pltpu.VMEM((batch, n_chunks, 2 * DH, CHUNK), BF16),
            pltpu.VMEM((batch, n_chunks, 2 * DH, DH), BF16),
            pltpu.VMEM((4 * batch, 1, tokens), F32),
            pltpu.VMEM((batch, 6 * DH, tokens), BF16),
            pltpu.VMEM((batch, n_chunks, DH, CHUNK), F32),
            pltpu.VMEM((batch, n_chunks, DH, CHUNK), F32),
            pltpu.VMEM((6 * DH, 2 * DH), F32),
            pltpu.VMEM((batch, *square), F32),
            pltpu.VMEM((batch, *square), F32),
            pltpu.VMEM((batch, *half), F32),
            pltpu.VMEM((batch, 2, 2, *half), F32),
            pltpu.VMEM((batch, 2, *half), F32),
            pltpu.VMEM((batch, 2 * DH, 6 * DH), BF16),
            pltpu.VMEM((batch, N_X, 2 * n_chunks, CHUNK), F32),
            pltpu.VMEM((batch, n_z, 2 * n_chunks, CHUNK), F32),
            pltpu.VMEM((batch, 2 * n_chunks, CHUNK), F32),
            pltpu.VMEM((batch, *square), F32),
            pltpu.VMEM((batch, 2, 2, *half), F32),
            pltpu.VMEM((batch, *square), F32),
            pltpu.VMEM((batch, 2, *half), F32),
            pltpu.VMEM((batch, 2, *half), F32),
            pltpu.VMEM((batch, 3, *half), F32),
            pltpu.VMEM((batch, 2, *half), F32),
            pltpu.SemaphoreType.DMA((4, 2)),
            pltpu.SemaphoreType.DMA((4,)),
            pltpu.SemaphoreType.DMA((11, 2)),
            pltpu.SemaphoreType.DMA((11, 2)),
            pltpu.SemaphoreType.DMA((2, 2)),
            pltpu.SemaphoreType.DMA((2, 2)),
        ]
        hbm = pl.BlockSpec(memory_space=pltpu.HBM)
        vmem = pl.BlockSpec(memory_space=pltpu.VMEM)
        return pl.pallas_call(
            functools.partial(kernel, N_X, n_z, tokens),
            out_shape=(
                jax.ShapeDtypeStruct(whole, F32),
                jax.ShapeDtypeStruct((batch, 1, DH, DH), F32),
            ),
            in_specs=[hbm] * 8,
            out_specs=(vmem, vmem),
            scratch_shapes=scratch,
            compiler_params=pltpu.CompilerParams(
                collective_id=0, has_side_effects=True, vmem_limit_bytes=50 * 2**20
            ),
            cost_estimate=pl.CostEstimate(
                flops=2 * 10**10, bytes_accessed=12 * 2**20, transcendentals=0
            ),
        )(
            query_rows, key_rows, value_rows, cotangent,
            *(
                pltpu.with_memory_space_constraint(small, pltpu.HBM)
                for small in (selector, level_table.T, span_length.T, norm_gain.reshape(1, DH))
            ),
        )

    return jax.shard_map(
        local,
        mesh=mesh,
        in_specs=(
            P(None, "seq", "head"),
            P(None, "seq", "head"),
            P(None, "seq", "head"),
            P(None, "seq", "head"),
            P(None, "head", "seq"),
            P(),
            P(None, "seq"),
            P("head"),
        ),
        out_specs=(P(None, "seq", "head"), P(None, "seq", None, "head")),
        check_vma=False,
    )
```

```python
import functools

import jax
import jax.numpy as jnp
from jax import lax
from jax.experimental import pallas as pl
from jax.experimental.pallas import tpu as pltpu
from jax.sharding import PartitionSpec as P

DH = 128
CHUNK = 256
WIDE = 1024
U_STATE = 8
U_LOCAL = 4
U_READ = 8
U_ATT = 8
N_X = 4
EPS = 1e-06
F32 = jnp.float32
BF16 = jnp.bfloat16


def split(x):
    high = x.astype(BF16)
    return high, (x - high.astype(F32)).astype(BF16)


def mm(a, b):
    return jnp.dot(a, b, preferred_element_type=F32)


def mm_nt(a, b):
    return lax.dot_general(a, b, (((1,), (1,)), ((), ())), preferred_element_type=F32)


def remote(src, dst, send_sem, recv_sem, device):
    return pltpu.make_async_remote_copy(
        src_ref=src,
        dst_ref=dst,
        send_sem=send_sem,
        recv_sem=recv_sem,
        device_id=device,
        device_id_type=pl.DeviceIdType.MESH,
    )


def kernel(
    n_x, n_z, tokens,
    q_hbm, k_hbm, v_hbm, c_hbm, sel_hbm, tab_hbm, span_hbm, gain_hbm,
    att_ref, sg_ref,
    sel_ref, tab_ref, span_ref, gain_ref,
    qb, kb, vb, cb, kh, kl, vt, pp, wrow, wq, comb, sc, gacc,
    st, b0, pair, b12, far_in, lb, x_in, z_in, coef, gr0, grh, t0, t1, r12, r_in, total,
    load_sem, small_sem, send_sem, recv_sem, h_send, h_recv,
):
    n_chunks = tokens // CHUNK
    half = DH // 2
    seq = lax.axis_index("seq")
    head = lax.axis_index("head")
    core = lax.rem(seq, 2)
    other = 1 - core
    chip = lax.div(seq, 2)
    mate = seq + 1 - 2 * core
    near = 2 * (chip + 1 - 2 * lax.rem(chip, 2)) + core
    far = 2 * (3 - chip) + core
    across = lax.rem(seq + 4, 8)
    x = lax.div(head, n_z)
    z = lax.rem(head, n_z)
    x_peers = [n_z * lax.rem(x + r, n_x) + z for r in range(1, n_x)]
    z_peers = [n_z * x + lax.rem(z + r, n_z) for r in range(1, n_z)]

    def to(peer):
        return {"seq": peer, "head": head}

    def along(peer):
        return {"seq": seq, "head": peer}

    peers = [to(p) for p in (mate, near, far, across)] + [along(p) for p in x_peers + z_peers]

    small = [
        pltpu.make_async_copy(src, dst, small_sem.at[i])
        for i, (src, dst) in enumerate(
            ((tab_hbm, tab_ref), (span_hbm, span_ref), (sel_hbm, sel_ref), (gain_hbm, gain_ref))
        )
    ]
    for copy in small:
        copy.start()
    loads = {}
    pairs = (("k", k_hbm, kb), ("v", v_hbm, vb), ("q", q_hbm, qb), ("c", c_hbm, cb))
    for first in (0, 2):
        for b in range(2):
            for i in (first, first + 1):
                name, src, dst = pairs[i]
                loads[name, b] = pltpu.make_async_copy(src.at[b], dst.at[b], load_sem.at[i, b])

    def load(names, b):
        for name in names:
            loads[name, b].start()

    load("kv", 0)
    load("kv", 1)

    barrier = pltpu.get_barrier_semaphore()
    for peer in peers:
        pl.semaphore_signal(barrier, 1, device_id=peer, device_id_type=pl.DeviceIdType.MESH)

    for copy in small:
        copy.wait()
    selector = [sel_ref[b] for b in range(2)]
    for level in range(4):
        on = 1 if level == 0 else lax.rem(lax.div(seq, 2 ** (level - 1)), 2)
        for b in range(2):
            row = jnp.zeros((1, tokens), F32)
            for choice in range(16):
                row = jnp.where(selector[b] == choice, tab_ref[level, choice], row)
            if level > 0:
                row = jnp.where(on == 1, row, 0.0)
            wrow[level * 2 + b] = row

    def lanes(n):
        return pl.ds(pl.multiple_of(n * CHUNK, CHUNK), CHUNK)

    def states(b):
        span = span_ref[0, b]

        def step(i, acc):
            for u in range(U_STATE):
                n = i * U_STATE + u
                rows = lanes(n)
                position = n * CHUNK + lax.broadcasted_iota(jnp.int32, (CHUNK, DH), 0)
                k_hi, k_lo = split(jnp.where(position < span, kb[b, rows, :], 0.0))
                kh[b, rows, :] = k_hi
                kl[b, rows, :] = k_lo
                v_hi, v_lo = split(vb[b, rows, :].T)
                v_two = jnp.concatenate([v_hi, v_lo], axis=0)
                vt[b, n] = v_two
                p_hi, p_lo = split(acc)
                pp[b, n] = jnp.concatenate([p_hi, p_lo], axis=0)
                out = mm(v_two, jnp.concatenate([k_hi, k_lo], axis=1))
                acc = acc + (out[:DH, :DH] + (out[:DH, DH:] + out[DH:, :DH]))
            return acc

        st[b] = lax.fori_loop(0, n_chunks // U_STATE, step, jnp.zeros((DH, DH), F32))

    def local_chunk(b, n):
        rows = lanes(n)
        q_t = qb[b, rows, :].T
        q_hi, q_lo = split(q_t)
        k_hi, k_lo = kh[b, rows, :], kl[b, rows, :]
        scores = mm(
            jnp.concatenate([k_hi, k_hi, k_lo], axis=1), jnp.concatenate([q_hi, q_lo, q_hi], axis=0)
        )
        key_at = lax.broadcasted_iota(jnp.int32, (CHUNK, CHUNK), 0)
        query_at = lax.broadcasted_iota(jnp.int32, (CHUNK, CHUNK), 1)
        s_hi, s_lo = split(jnp.where(key_at <= query_at, scores, 0.0))
        v_two, p_two = vt[b, n], pp[b, n]
        out = mm(
            jnp.concatenate([v_two, v_two, p_two, p_two], axis=1),
            jnp.concatenate([s_hi, s_lo, q_hi, q_lo], axis=0),
        )
        comb[b, n] = (out[:DH] + out[DH:]) * wrow[b, :, rows]
        for level in range(3):
            w_hi, w_lo = split(q_t * wrow[2 * (level + 1) + b, :, rows])
            wq[b, level * DH : (level + 1) * DH, rows] = w_hi
            wq[b, (3 + level) * DH : (4 + level) * DH, rows] = w_lo
        sc[b, n] = (cb[b, rows, :] * gain_ref[...]).T

    def local_chunks(b, low, high):
        @pl.loop(0, (high - low) // U_LOCAL)
        def _(i):
            for u in range(U_LOCAL):
                local_chunk(b, low + i * U_LOCAL + u)

    s1, s2, s4 = {}, {}, {}
    for b in range(2):
        loads["k", b].wait()
        loads["v", b].wait()
        load("qc", b)
        states(b)
        if b == 0:
            pl.semaphore_wait(barrier, len(peers))
        s1[b] = remote(st.at[b], b0.at[b], send_sem.at[0, b], recv_sem.at[0, b], to(mate))
        s1[b].start()

    def sum_pair(b):
        s1[b].wait_recv()
        mine = pl.ds(pl.multiple_of(core * half, half), half)
        pair[b] = st[b, mine, :] + b0[b, mine, :]
        s2[b] = [
            remote(pair.at[b], far_in.at[b, 0], send_sem.at[1, b], recv_sem.at[1, b], to(across)),
            remote(pair.at[b], far_in.at[b, 1], send_sem.at[2, b], recv_sem.at[2, b], to(far)),
            remote(pair.at[b], b12.at[b, core, 0], send_sem.at[3, b], recv_sem.at[3, b], to(near)),
        ]
        for copy in s2[b]:
            copy.start()

    def sum_quad(b):
        for copy in s2[b]:
            copy.wait_recv()
        b12[b, core, 1] = far_in[b, 0] + far_in[b, 1]
        s4[b] = remote(
            b12.at[b, core], b12.at[b, core], send_sem.at[4, b], recv_sem.at[4, b], to(mate)
        )
        s4[b].start()

    middle = n_chunks // 2
    sum_pair(0)
    loads["q", 0].wait()
    loads["c", 0].wait()
    local_chunks(0, 0, middle)
    sum_pair(1)
    local_chunks(0, middle, n_chunks)
    loads["q", 1].wait()
    loads["c", 1].wait()
    local_chunks(1, 0, middle)
    sum_quad(0)
    local_chunks(1, middle, n_chunks)

    def reads(b, sums):
        halves = [split(b0[b])]
        for level in range(2):
            halves.append(split(jnp.concatenate([b12[b, 0, level], b12[b, 1, level]], axis=0)))
        high = jnp.concatenate([h[0] for h in halves], axis=1)
        low = jnp.concatenate([h[1] for h in halves], axis=1)
        lb[b, :DH] = jnp.concatenate([high, high], axis=1)
        lb[b, DH:] = jnp.concatenate([low, low], axis=1)

        @pl.loop(0, n_chunks // U_READ)
        def _(i):
            for u in range(U_READ):
                n = i * U_READ + u
                out = mm(lb[b], wq[b, :, lanes(n)])
                mixed = comb[b, n] + (out[:DH] + out[DH:])
                comb[b, n] = mixed
                sums[pl.ds(n, 1), :] = jnp.sum(mixed * mixed, axis=0, keepdims=True)
                sums[pl.ds(n_chunks + n, 1), :] = jnp.sum(sc[b, n] * mixed, axis=0, keepdims=True)

    def arrived(buffer, count, sem):
        window = buffer.at[pl.ds(0, count)]
        pltpu.make_async_copy(window, window, sem).wait()

    z_order = sorted(range(1, n_z), key=lambda r: -min(r, n_z - r))
    x_stage = (x_in, x, [x_peers[r] for r in (1, 0, 2)], n_x - 1)
    z_stage = (z_in, z, [z_peers[r - 1] for r in z_order], n_z - 1)
    stages = ((x_stage, z_stage), (z_stage, x_stage))

    def send_sums(b, step):
        buffer, mine, others, _ = stages[b][step]
        for peer in others:
            remote(
                buffer.at[b, mine], buffer.at[b, mine], h_send.at[step, b], h_recv.at[step, b],
                along(peer),
            ).start()

    def receive_sums(b, step):
        buffer, _, _, count = stages[b][step]
        arrived(buffer.at[b], count, h_recv.at[step, b])
        return jnp.sum(buffer[b], axis=0)

    def pass_on(b):
        partial = receive_sums(b, 0)
        buffer, mine, _, _ = stages[b][1]
        buffer[b, mine] = partial
        send_sums(b, 1)

    def coefficients(b):
        whole = receive_sums(b, 1)
        width = n_x * n_z * DH
        inverse = lax.rsqrt(whole[:n_chunks] / width + EPS)
        coef[b, :n_chunks] = inverse
        coef[b, n_chunks:] = inverse * inverse * inverse * whole[n_chunks:] / width

    for b in range(2):
        s4[b].wait_recv()
        buffer, mine, _, _ = stages[b][0]
        reads(b, buffer.at[b, mine])
        send_sums(b, 0)
        if b == 0:
            sum_quad(1)
    pass_on(0)
    pass_on(1)

    def level_grads(b):
        gacc[...] = jnp.zeros_like(gacc)
        pieces = WIDE // CHUNK

        @pl.loop(0, tokens // WIDE)
        def _(n):
            parts = []
            for i in range(pieces):
                m = n * pieces + i
                grad = sc[b, m] * coef[b, pl.ds(m, 1), :] - comb[b, m] * coef[b, pl.ds(n_chunks + m, 1), :]
                parts.append(jnp.concatenate(split(grad), axis=0))
            rows = pl.ds(pl.multiple_of(n * WIDE, WIDE), WIDE)
            gacc[...] += mm_nt(wq[b, :, rows], jnp.concatenate(parts, axis=1))

        for level in range(3):
            top = slice(level * DH, (level + 1) * DH)
            bottom = slice((3 + level) * DH, (4 + level) * DH)
            grad = gacc[top, :DH] + (gacc[top, DH:] + gacc[bottom, :DH])
            if level == 0:
                gr0[b] = grad
            else:
                grh[b, 0, level - 1] = grad[:half]
                grh[b, 1, level - 1] = grad[half:]

    def attended(b):
        @pl.loop(0, n_chunks // U_ATT)
        def _(i):
            for u in range(U_ATT):
                n = i * U_ATT + u
                att_ref[b, lanes(n), :] = (comb[b, n] * coef[b, pl.ds(n, 1), :]).T * gain_ref[...]

    g1, g2, g4 = {}, {}, {}

    def send_mate(b):
        g1[b] = [
            remote(grh.at[b, other], t1.at[b], send_sem.at[5, b], recv_sem.at[5, b], to(mate)),
            remote(gr0.at[b], t0.at[b], send_sem.at[6, b], recv_sem.at[6, b], to(mate)),
        ]
        for copy in g1[b]:
            copy.start()

    def send_chips(b):
        g1[b][0].wait_recv()
        r12[b] = grh[b, core] + t1[b]
        g2[b] = [
            remote(r12.at[b, 1], r_in.at[b, 0], send_sem.at[7, b], recv_sem.at[7, b], to(across)),
            remote(r12.at[b, 1], r_in.at[b, 1], send_sem.at[8, b], recv_sem.at[8, b], to(far)),
            remote(r12.at[b, 0], r_in.at[b, 2], send_sem.at[9, b], recv_sem.at[9, b], to(near)),
        ]
        for copy in g2[b]:
            copy.start()

    def send_total(b):
        for copy in g2[b]:
            copy.wait_recv()
        total[b, core] = r_in[b, 0] + r_in[b, 1] + r_in[b, 2]
        g4[b] = remote(
            total.at[b, core], total.at[b, core], send_sem.at[10, b], recv_sem.at[10, b], to(mate)
        )
        g4[b].start()

    for b in range(2):
        coefficients(b)
        level_grads(b)
        send_mate(b)
        attended(b)
        send_chips(b)
    send_total(0)
    send_total(1)
    for b in range(2):
        g1[b][1].wait_recv()
        g4[b].wait_recv()
        sg_ref[b, 0, :half] = total[b, 0] + t0[b, :half]
        sg_ref[b, 0, half:] = total[b, 1] + t0[b, half:]

    for b in range(2):
        for copy in (s1[b], s4[b], g4[b], *s2[b], *g1[b], *g2[b]):
            copy.wait_send()
        for step in range(2):
            buffer, _, _, count = stages[b][step]
            arrived(buffer.at[b], count, h_send.at[step, b])


def solution(mesh):
    n_z = mesh.shape["head"] // N_X

    def local(
        query_rows, key_rows, value_rows, cotangent, selector, level_table, span_length, norm_gain
    ):
        batch, tokens, _ = query_rows.shape
        n_chunks = tokens // CHUNK
        square = (DH, DH)
        half = (DH // 2, DH)
        whole = (batch, tokens, DH)
        scratch = [
            pltpu.VMEM((batch, 1, tokens), jnp.int32),
            pltpu.SMEM((4, 16), F32),
            pltpu.SMEM((1, batch), jnp.int32),
            pltpu.VMEM((1, DH), F32),
        ]
        scratch += [pltpu.VMEM(whole, F32) for _ in range(4)]
        scratch += [
            pltpu.VMEM(whole, BF16),
            pltpu.VMEM(whole, BF16),
            pltpu.VMEM((batch, n_chunks, 2 * DH, CHUNK), BF16),
            pltpu.VMEM((batch, n_chunks, 2 * DH, DH), BF16),
            pltpu.VMEM((4 * batch, 1, tokens), F32),
            pltpu.VMEM((batch, 6 * DH, tokens), BF16),
            pltpu.VMEM((batch, n_chunks, DH, CHUNK), F32),
            pltpu.VMEM((batch, n_chunks, DH, CHUNK), F32),
            pltpu.VMEM((6 * DH, 2 * DH), F32),
            pltpu.VMEM((batch, *square), F32),
            pltpu.VMEM((batch, *square), F32),
            pltpu.VMEM((batch, *half), F32),
            pltpu.VMEM((batch, 2, 2, *half), F32),
            pltpu.VMEM((batch, 2, *half), F32),
            pltpu.VMEM((batch, 2 * DH, 6 * DH), BF16),
            pltpu.VMEM((batch, N_X, 2 * n_chunks, CHUNK), F32),
            pltpu.VMEM((batch, n_z, 2 * n_chunks, CHUNK), F32),
            pltpu.VMEM((batch, 2 * n_chunks, CHUNK), F32),
            pltpu.VMEM((batch, *square), F32),
            pltpu.VMEM((batch, 2, 2, *half), F32),
            pltpu.VMEM((batch, *square), F32),
            pltpu.VMEM((batch, 2, *half), F32),
            pltpu.VMEM((batch, 2, *half), F32),
            pltpu.VMEM((batch, 3, *half), F32),
            pltpu.VMEM((batch, 2, *half), F32),
            pltpu.SemaphoreType.DMA((4, 2)),
            pltpu.SemaphoreType.DMA((4,)),
            pltpu.SemaphoreType.DMA((11, 2)),
            pltpu.SemaphoreType.DMA((11, 2)),
            pltpu.SemaphoreType.DMA((2, 2)),
            pltpu.SemaphoreType.DMA((2, 2)),
        ]
        hbm = pl.BlockSpec(memory_space=pltpu.HBM)
        vmem = pl.BlockSpec(memory_space=pltpu.VMEM)
        return pl.pallas_call(
            functools.partial(kernel, N_X, n_z, tokens),
            out_shape=(
                jax.ShapeDtypeStruct(whole, F32),
                jax.ShapeDtypeStruct((batch, 1, DH, DH), F32),
            ),
            in_specs=[hbm] * 8,
            out_specs=(vmem, vmem),
            scratch_shapes=scratch,
            compiler_params=pltpu.CompilerParams(
                collective_id=0, has_side_effects=True, vmem_limit_bytes=50 * 2**20
            ),
            cost_estimate=pl.CostEstimate(
                flops=2 * 10**10, bytes_accessed=12 * 2**20, transcendentals=0
            ),
        )(
            query_rows, key_rows, value_rows, cotangent,
            *(
                pltpu.with_memory_space_constraint(small, pltpu.HBM)
                for small in (selector, level_table.T, span_length.T, norm_gain.reshape(1, DH))
            ),
        )

    return jax.shard_map(
        local,
        mesh=mesh,
        in_specs=(
            P(None, "seq", "head"),
            P(None, "seq", "head"),
            P(None, "seq", "head"),
            P(None, "seq", "head"),
            P(None, "head", "seq"),
            P(),
            P(None, "seq"),
            P("head"),
        ),
        out_specs=(P(None, "seq", "head"), P(None, "seq", None, "head")),
        check_vma=False,
    )
```

```python
import functools

import jax
import jax.numpy as jnp
from jax import lax
from jax.experimental import pallas as pl
from jax.experimental.pallas import tpu as pltpu
from jax.sharding import PartitionSpec as P

DH = 128
CHUNK = 256
WIDE = 1024
U_STATE = 8
U_LOCAL = 4
U_READ = 8
U_ATT = 4
N_X = 4
EPS = 1e-06
F32 = jnp.float32
BF16 = jnp.bfloat16


def split(x):
    high = x.astype(BF16)
    return high, (x - high.astype(F32)).astype(BF16)


def mm(a, b):
    return jnp.dot(a, b, preferred_element_type=F32)


def mm_nt(a, b):
    return lax.dot_general(a, b, (((1,), (1,)), ((), ())), preferred_element_type=F32)


def remote(src, dst, send_sem, recv_sem, device):
    return pltpu.make_async_remote_copy(
        src_ref=src,
        dst_ref=dst,
        send_sem=send_sem,
        recv_sem=recv_sem,
        device_id=device,
        device_id_type=pl.DeviceIdType.MESH,
    )


def kernel(
    n_x, n_z, tokens,
    q_hbm, k_hbm, v_hbm, c_hbm, sel_hbm, tab_hbm, span_hbm, gain_hbm,
    att_ref, sg_ref,
    sel_ref, tab_ref, span_ref, gain_ref,
    qb, kb, vb, cb, kh, kl, vt, pp, wrow, wq, comb, sc, gacc,
    st, b0, pair, b12, far_in, lb, x_in, z_in, coef, gr0, grh, t0, t1, r12, r_in, total,
    load_sem, small_sem, send_sem, recv_sem, h_send, h_recv,
):
    n_chunks = tokens // CHUNK
    half = DH // 2
    seq = lax.axis_index("seq")
    head = lax.axis_index("head")
    core = lax.rem(seq, 2)
    other = 1 - core
    chip = lax.div(seq, 2)
    mate = seq + 1 - 2 * core
    near = 2 * (chip + 1 - 2 * lax.rem(chip, 2)) + core
    far = 2 * (3 - chip) + core
    across = lax.rem(seq + 4, 8)
    x = lax.div(head, n_z)
    z = lax.rem(head, n_z)
    x_peers = [n_z * lax.rem(x + r, n_x) + z for r in range(1, n_x)]
    z_peers = [n_z * x + lax.rem(z + r, n_z) for r in range(1, n_z)]

    def to(peer):
        return {"seq": peer, "head": head}

    def along(peer):
        return {"seq": seq, "head": peer}

    peers = [to(p) for p in (mate, near, far, across)] + [along(p) for p in x_peers + z_peers]

    small = [
        pltpu.make_async_copy(src, dst, small_sem.at[i])
        for i, (src, dst) in enumerate(
            ((tab_hbm, tab_ref), (span_hbm, span_ref), (sel_hbm, sel_ref), (gain_hbm, gain_ref))
        )
    ]
    for copy in small:
        copy.start()
    loads = {}
    pairs = (("k", k_hbm, kb), ("v", v_hbm, vb), ("q", q_hbm, qb), ("c", c_hbm, cb))
    for first in (0, 2):
        for b in range(2):
            for i in (first, first + 1):
                name, src, dst = pairs[i]
                loads[name, b] = pltpu.make_async_copy(src.at[b], dst.at[b], load_sem.at[i, b])

    def load(names, b):
        for name in names:
            loads[name, b].start()

    load("kv", 0)
    load("kv", 1)

    barrier = pltpu.get_barrier_semaphore()
    for peer in peers:
        pl.semaphore_signal(barrier, 1, device_id=peer, device_id_type=pl.DeviceIdType.MESH)

    for copy in small:
        copy.wait()
    selector = [sel_ref[b] for b in range(2)]
    for level in range(4):
        on = 1 if level == 0 else lax.rem(lax.div(seq, 2 ** (level - 1)), 2)
        for b in range(2):
            row = jnp.zeros((1, tokens), F32)
            for choice in range(16):
                row = jnp.where(selector[b] == choice, tab_ref[level, choice], row)
            if level > 0:
                row = jnp.where(on == 1, row, 0.0)
            wrow[level * 2 + b] = row

    def lanes(n):
        return pl.ds(pl.multiple_of(n * CHUNK, CHUNK), CHUNK)

    def states(b):
        span = span_ref[0, b]

        def step(i, acc):
            for u in range(U_STATE):
                n = i * U_STATE + u
                rows = lanes(n)
                position = n * CHUNK + lax.broadcasted_iota(jnp.int32, (CHUNK, DH), 0)
                k_hi, k_lo = split(jnp.where(position < span, kb[b, rows, :], 0.0))
                kh[b, rows, :] = k_hi
                kl[b, rows, :] = k_lo
                v_hi, v_lo = split(vb[b, rows, :].T)
                v_two = jnp.concatenate([v_hi, v_lo], axis=0)
                vt[b, n] = v_two
                p_hi, p_lo = split(acc)
                pp[b, n] = jnp.concatenate([p_hi, p_lo], axis=0)
                out = mm(v_two, jnp.concatenate([k_hi, k_lo], axis=1))
                acc = acc + (out[:DH, :DH] + (out[:DH, DH:] + out[DH:, :DH]))
            return acc

        st[b] = lax.fori_loop(0, n_chunks // U_STATE, step, jnp.zeros((DH, DH), F32))

    def local_chunk(b, n):
        rows = lanes(n)
        q_t = qb[b, rows, :].T
        q_hi, q_lo = split(q_t)
        k_hi, k_lo = kh[b, rows, :], kl[b, rows, :]
        scores = mm(
            jnp.concatenate([k_hi, k_hi, k_lo], axis=1), jnp.concatenate([q_hi, q_lo, q_hi], axis=0)
        )
        key_at = lax.broadcasted_iota(jnp.int32, (CHUNK, CHUNK), 0)
        query_at = lax.broadcasted_iota(jnp.int32, (CHUNK, CHUNK), 1)
        s_hi, s_lo = split(jnp.where(key_at <= query_at, scores, 0.0))
        v_two, p_two = vt[b, n], pp[b, n]
        out = mm(
            jnp.concatenate([v_two, v_two, p_two, p_two], axis=1),
            jnp.concatenate([s_hi, s_lo, q_hi, q_lo], axis=0),
        )
        comb[b, n] = (out[:DH] + out[DH:]) * wrow[b, :, rows]
        for level in range(3):
            w_hi, w_lo = split(q_t * wrow[2 * (level + 1) + b, :, rows])
            wq[b, level * DH : (level + 1) * DH, rows] = w_hi
            wq[b, (3 + level) * DH : (4 + level) * DH, rows] = w_lo
        sc[b, n] = (cb[b, rows, :] * gain_ref[...]).T

    def local_chunks(b, low, high):
        @pl.loop(0, (high - low) // U_LOCAL)
        def _(i):
            for u in range(U_LOCAL):
                local_chunk(b, low + i * U_LOCAL + u)

    s1, s2, s4 = {}, {}, {}
    for b in range(2):
        loads["k", b].wait()
        loads["v", b].wait()
        load("qc", b)
        states(b)
        if b == 0:
            pl.semaphore_wait(barrier, len(peers))
        s1[b] = remote(st.at[b], b0.at[b], send_sem.at[0, b], recv_sem.at[0, b], to(mate))
        s1[b].start()

    def sum_pair(b):
        s1[b].wait_recv()
        mine = pl.ds(pl.multiple_of(core * half, half), half)
        pair[b] = st[b, mine, :] + b0[b, mine, :]
        s2[b] = [
            remote(pair.at[b], far_in.at[b, 0], send_sem.at[1, b], recv_sem.at[1, b], to(across)),
            remote(pair.at[b], far_in.at[b, 1], send_sem.at[2, b], recv_sem.at[2, b], to(far)),
            remote(pair.at[b], b12.at[b, core, 0], send_sem.at[3, b], recv_sem.at[3, b], to(near)),
        ]
        for copy in s2[b]:
            copy.start()

    def sum_quad(b):
        for copy in s2[b]:
            copy.wait_recv()
        b12[b, core, 1] = far_in[b, 0] + far_in[b, 1]
        s4[b] = remote(
            b12.at[b, core], b12.at[b, core], send_sem.at[4, b], recv_sem.at[4, b], to(mate)
        )
        s4[b].start()

    middle = n_chunks // 2
    sum_pair(0)
    loads["q", 0].wait()
    loads["c", 0].wait()
    local_chunks(0, 0, middle)
    sum_pair(1)
    local_chunks(0, middle, n_chunks)
    loads["q", 1].wait()
    loads["c", 1].wait()
    local_chunks(1, 0, middle)
    sum_quad(0)
    local_chunks(1, middle, n_chunks)

    def reads(b, sums):
        halves = [split(b0[b])]
        for level in range(2):
            halves.append(split(jnp.concatenate([b12[b, 0, level], b12[b, 1, level]], axis=0)))
        high = jnp.concatenate([h[0] for h in halves], axis=1)
        low = jnp.concatenate([h[1] for h in halves], axis=1)
        lb[b, :DH] = jnp.concatenate([high, high], axis=1)
        lb[b, DH:] = jnp.concatenate([low, low], axis=1)

        @pl.loop(0, n_chunks // U_READ)
        def _(i):
            for u in range(U_READ):
                n = i * U_READ + u
                out = mm(lb[b], wq[b, :, lanes(n)])
                mixed = comb[b, n] + (out[:DH] + out[DH:])
                comb[b, n] = mixed
                sums[pl.ds(n, 1), :] = jnp.sum(mixed * mixed, axis=0, keepdims=True)
                sums[pl.ds(n_chunks + n, 1), :] = jnp.sum(sc[b, n] * mixed, axis=0, keepdims=True)

    def arrived(buffer, count, sem):
        window = buffer.at[pl.ds(0, count)]
        pltpu.make_async_copy(window, window, sem).wait()

    z_order = sorted(range(1, n_z), key=lambda r: -min(r, n_z - r))
    x_stage = (x_in, x, [x_peers[r] for r in (1, 0, 2)], n_x - 1)
    z_stage = (z_in, z, [z_peers[r - 1] for r in z_order], n_z - 1)
    stages = ((z_stage, x_stage), (x_stage, z_stage))

    def send_sums(b, step):
        buffer, mine, others, _ = stages[b][step]
        for peer in others:
            remote(
                buffer.at[b, mine], buffer.at[b, mine], h_send.at[step, b], h_recv.at[step, b],
                along(peer),
            ).start()

    def receive_sums(b, step):
        buffer, _, _, count = stages[b][step]
        arrived(buffer.at[b], count, h_recv.at[step, b])
        return jnp.sum(buffer[b], axis=0)

    def pass_on(b):
        partial = receive_sums(b, 0)
        buffer, mine, _, _ = stages[b][1]
        buffer[b, mine] = partial
        send_sums(b, 1)

    def coefficients(b):
        whole = receive_sums(b, 1)
        width = n_x * n_z * DH
        inverse = lax.rsqrt(whole[:n_chunks] / width + EPS)
        coef[b, :n_chunks] = inverse
        coef[b, n_chunks:] = inverse * inverse * inverse * whole[n_chunks:] / width

    for b in range(2):
        s4[b].wait_recv()
        buffer, mine, _, _ = stages[b][0]
        reads(b, buffer.at[b, mine])
        send_sums(b, 0)
        if b == 0:
            sum_quad(1)
    pass_on(0)
    pass_on(1)

    def level_grads(b):
        gacc[...] = jnp.zeros_like(gacc)
        pieces = WIDE // CHUNK

        @pl.loop(0, tokens // WIDE)
        def _(n):
            parts = []
            for i in range(pieces):
                m = n * pieces + i
                grad = sc[b, m] * coef[b, pl.ds(m, 1), :] - comb[b, m] * coef[b, pl.ds(n_chunks + m, 1), :]
                parts.append(jnp.concatenate(split(grad), axis=0))
            rows = pl.ds(pl.multiple_of(n * WIDE, WIDE), WIDE)
            gacc[...] += mm_nt(wq[b, :, rows], jnp.concatenate(parts, axis=1))

        for level in range(3):
            top = slice(level * DH, (level + 1) * DH)
            bottom = slice((3 + level) * DH, (4 + level) * DH)
            grad = gacc[top, :DH] + (gacc[top, DH:] + gacc[bottom, :DH])
            if level == 0:
                gr0[b] = grad
            else:
                grh[b, 0, level - 1] = grad[:half]
                grh[b, 1, level - 1] = grad[half:]

    def attended(b):
        @pl.loop(0, n_chunks // U_ATT)
        def _(i):
            for u in range(U_ATT):
                n = i * U_ATT + u
                att_ref[b, lanes(n), :] = (comb[b, n] * coef[b, pl.ds(n, 1), :]).T * gain_ref[...]

    g1, g2, g4 = {}, {}, {}

    def send_mate(b):
        g1[b] = [
            remote(grh.at[b, other], t1.at[b], send_sem.at[5, b], recv_sem.at[5, b], to(mate)),
            remote(gr0.at[b], t0.at[b], send_sem.at[6, b], recv_sem.at[6, b], to(mate)),
        ]
        for copy in g1[b]:
            copy.start()

    def send_chips(b):
        g1[b][0].wait_recv()
        r12[b] = grh[b, core] + t1[b]
        g2[b] = [
            remote(r12.at[b, 1], r_in.at[b, 0], send_sem.at[7, b], recv_sem.at[7, b], to(across)),
            remote(r12.at[b, 1], r_in.at[b, 1], send_sem.at[8, b], recv_sem.at[8, b], to(far)),
            remote(r12.at[b, 0], r_in.at[b, 2], send_sem.at[9, b], recv_sem.at[9, b], to(near)),
        ]
        for copy in g2[b]:
            copy.start()

    def send_total(b):
        for copy in g2[b]:
            copy.wait_recv()
        total[b, core] = r_in[b, 0] + r_in[b, 1] + r_in[b, 2]
        g4[b] = remote(
            total.at[b, core], total.at[b, core], send_sem.at[10, b], recv_sem.at[10, b], to(mate)
        )
        g4[b].start()

    for b in range(2):
        coefficients(b)
        level_grads(b)
        send_mate(b)
        attended(b)
        send_chips(b)
    send_total(0)
    send_total(1)
    for b in range(2):
        g1[b][1].wait_recv()
        g4[b].wait_recv()
        sg_ref[b, 0, :half] = total[b, 0] + t0[b, :half]
        sg_ref[b, 0, half:] = total[b, 1] + t0[b, half:]

    for b in range(2):
        for copy in (s1[b], s4[b], g4[b], *s2[b], *g1[b], *g2[b]):
            copy.wait_send()
        for step in range(2):
            buffer, _, _, count = stages[b][step]
            arrived(buffer.at[b], count, h_send.at[step, b])


def solution(mesh):
    n_z = mesh.shape["head"] // N_X

    def local(
        query_rows, key_rows, value_rows, cotangent, selector, level_table, span_length, norm_gain
    ):
        batch, tokens, _ = query_rows.shape
        n_chunks = tokens // CHUNK
        square = (DH, DH)
        half = (DH // 2, DH)
        whole = (batch, tokens, DH)
        scratch = [
            pltpu.VMEM((batch, 1, tokens), jnp.int32),
            pltpu.SMEM((4, 16), F32),
            pltpu.SMEM((1, batch), jnp.int32),
            pltpu.VMEM((1, DH), F32),
        ]
        scratch += [pltpu.VMEM(whole, F32) for _ in range(4)]
        scratch += [
            pltpu.VMEM(whole, BF16),
            pltpu.VMEM(whole, BF16),
            pltpu.VMEM((batch, n_chunks, 2 * DH, CHUNK), BF16),
            pltpu.VMEM((batch, n_chunks, 2 * DH, DH), BF16),
            pltpu.VMEM((4 * batch, 1, tokens), F32),
            pltpu.VMEM((batch, 6 * DH, tokens), BF16),
            pltpu.VMEM((batch, n_chunks, DH, CHUNK), F32),
            pltpu.VMEM((batch, n_chunks, DH, CHUNK), F32),
            pltpu.VMEM((6 * DH, 2 * DH), F32),
            pltpu.VMEM((batch, *square), F32),
            pltpu.VMEM((batch, *square), F32),
            pltpu.VMEM((batch, *half), F32),
            pltpu.VMEM((batch, 2, 2, *half), F32),
            pltpu.VMEM((batch, 2, *half), F32),
            pltpu.VMEM((batch, 2 * DH, 6 * DH), BF16),
            pltpu.VMEM((batch, N_X, 2 * n_chunks, CHUNK), F32),
            pltpu.VMEM((batch, n_z, 2 * n_chunks, CHUNK), F32),
            pltpu.VMEM((batch, 2 * n_chunks, CHUNK), F32),
            pltpu.VMEM((batch, *square), F32),
            pltpu.VMEM((batch, 2, 2, *half), F32),
            pltpu.VMEM((batch, *square), F32),
            pltpu.VMEM((batch, 2, *half), F32),
            pltpu.VMEM((batch, 2, *half), F32),
            pltpu.VMEM((batch, 3, *half), F32),
            pltpu.VMEM((batch, 2, *half), F32),
            pltpu.SemaphoreType.DMA((4, 2)),
            pltpu.SemaphoreType.DMA((4,)),
            pltpu.SemaphoreType.DMA((11, 2)),
            pltpu.SemaphoreType.DMA((11, 2)),
            pltpu.SemaphoreType.DMA((2, 2)),
            pltpu.SemaphoreType.DMA((2, 2)),
        ]
        hbm = pl.BlockSpec(memory_space=pltpu.HBM)
        vmem = pl.BlockSpec(memory_space=pltpu.VMEM)
        return pl.pallas_call(
            functools.partial(kernel, N_X, n_z, tokens),
            out_shape=(
                jax.ShapeDtypeStruct(whole, F32),
                jax.ShapeDtypeStruct((batch, 1, DH, DH), F32),
            ),
            in_specs=[hbm] * 8,
            out_specs=(vmem, vmem),
            scratch_shapes=scratch,
            compiler_params=pltpu.CompilerParams(
                collective_id=0, has_side_effects=True, vmem_limit_bytes=50 * 2**20
            ),
            cost_estimate=pl.CostEstimate(
                flops=2 * 10**10, bytes_accessed=12 * 2**20, transcendentals=0
            ),
        )(
            query_rows, key_rows, value_rows, cotangent,
            *(
                pltpu.with_memory_space_constraint(small, pltpu.HBM)
                for small in (selector, level_table.T, span_length.T, norm_gain.reshape(1, DH))
            ),
        )

    return jax.shard_map(
        local,
        mesh=mesh,
        in_specs=(
            P(None, "seq", "head"),
            P(None, "seq", "head"),
            P(None, "seq", "head"),
            P(None, "seq", "head"),
            P(None, "head", "seq"),
            P(),
            P(None, "seq"),
            P("head"),
        ),
        out_specs=(P(None, "seq", "head"), P(None, "seq", None, "head")),
        check_vma=False,
    )
```

```python
import functools

import jax
import jax.numpy as jnp
from jax import lax
from jax.experimental import pallas as pl
from jax.experimental.pallas import tpu as pltpu
from jax.sharding import PartitionSpec as P

DH = 128
CHUNK = 256
WIDE = 1024
U_STATE = 8
U_LOCAL = 4
U_READ = 8
U_ATT = 4
N_X = 4
EPS = 1e-06
F32 = jnp.float32
BF16 = jnp.bfloat16


def split(x):
    high = x.astype(BF16)
    return high, (x - high.astype(F32)).astype(BF16)


def mm(a, b):
    return jnp.dot(a, b, preferred_element_type=F32)


def mm_nt(a, b):
    return lax.dot_general(a, b, (((1,), (1,)), ((), ())), preferred_element_type=F32)


def remote(src, dst, send_sem, recv_sem, device):
    return pltpu.make_async_remote_copy(
        src_ref=src,
        dst_ref=dst,
        send_sem=send_sem,
        recv_sem=recv_sem,
        device_id=device,
        device_id_type=pl.DeviceIdType.MESH,
    )


def kernel(
    n_x, n_z, tokens,
    q_hbm, k_hbm, v_hbm, c_hbm, sel_hbm, tab_hbm, span_hbm, gain_hbm,
    att_ref, sg_ref,
    sel_ref, tab_ref, span_ref, gain_ref,
    qb, kb, vb, cb, kh, kl, vt, pp, wrow, wq, comb, sc, gacc,
    st, b0, pair, b12, far_in, lb, x_in, z_in, coef, gr0, grh, t0, t1, r12, r_in, total,
    load_sem, small_sem, send_sem, recv_sem, h_send, h_recv,
):
    n_chunks = tokens // CHUNK
    half = DH // 2
    seq = lax.axis_index("seq")
    head = lax.axis_index("head")
    core = lax.rem(seq, 2)
    other = 1 - core
    chip = lax.div(seq, 2)
    mate = seq + 1 - 2 * core
    near = 2 * (chip + 1 - 2 * lax.rem(chip, 2)) + core
    far = 2 * (3 - chip) + core
    across = lax.rem(seq + 4, 8)
    x = lax.div(head, n_z)
    z = lax.rem(head, n_z)
    x_peers = [n_z * lax.rem(x + r, n_x) + z for r in range(1, n_x)]
    z_peers = [n_z * x + lax.rem(z + r, n_z) for r in range(1, n_z)]

    def to(peer):
        return {"seq": peer, "head": head}

    def along(peer):
        return {"seq": seq, "head": peer}

    peers = [to(p) for p in (mate, near, far, across)] + [along(p) for p in x_peers + z_peers]

    small = [
        pltpu.make_async_copy(src, dst, small_sem.at[i])
        for i, (src, dst) in enumerate(
            ((tab_hbm, tab_ref), (span_hbm, span_ref), (sel_hbm, sel_ref), (gain_hbm, gain_ref))
        )
    ]
    for copy in small:
        copy.start()
    loads = {}
    pairs = (("k", k_hbm, kb), ("v", v_hbm, vb), ("q", q_hbm, qb), ("c", c_hbm, cb))
    for first in (0, 2):
        for b in range(2):
            for i in (first, first + 1):
                name, src, dst = pairs[i]
                loads[name, b] = pltpu.make_async_copy(src.at[b], dst.at[b], load_sem.at[i, b])

    def load(names, b):
        for name in names:
            loads[name, b].start()

    load("kv", 0)
    load("kv", 1)

    barrier = pltpu.get_barrier_semaphore()
    for peer in peers:
        pl.semaphore_signal(barrier, 1, device_id=peer, device_id_type=pl.DeviceIdType.MESH)

    for copy in small:
        copy.wait()
    selector = [sel_ref[b] for b in range(2)]
    for level in range(4):
        on = 1 if level == 0 else lax.rem(lax.div(seq, 2 ** (level - 1)), 2)
        for b in range(2):
            row = jnp.zeros((1, tokens), F32)
            for choice in range(16):
                row = jnp.where(selector[b] == choice, tab_ref[level, choice], row)
            if level > 0:
                row = jnp.where(on == 1, row, 0.0)
            wrow[level * 2 + b] = row

    def lanes(n):
        return pl.ds(pl.multiple_of(n * CHUNK, CHUNK), CHUNK)

    def states(b):
        span = span_ref[0, b]

        def step(i, acc):
            for u in range(U_STATE):
                n = i * U_STATE + u
                rows = lanes(n)
                position = n * CHUNK + lax.broadcasted_iota(jnp.int32, (CHUNK, DH), 0)
                k_hi, k_lo = split(jnp.where(position < span, kb[b, rows, :], 0.0))
                kh[b, rows, :] = k_hi
                kl[b, rows, :] = k_lo
                v_hi, v_lo = split(vb[b, rows, :].T)
                v_two = jnp.concatenate([v_hi, v_lo], axis=0)
                vt[b, n] = v_two
                p_hi, p_lo = split(acc)
                pp[b, n] = jnp.concatenate([p_hi, p_lo], axis=0)
                out = mm(v_two, jnp.concatenate([k_hi, k_lo], axis=1))
                acc = acc + (out[:DH, :DH] + (out[:DH, DH:] + out[DH:, :DH]))
            return acc

        st[b] = lax.fori_loop(0, n_chunks // U_STATE, step, jnp.zeros((DH, DH), F32))

    def local_chunk(b, n):
        rows = lanes(n)
        q_t = qb[b, rows, :].T
        q_hi, q_lo = split(q_t)
        k_hi, k_lo = kh[b, rows, :], kl[b, rows, :]
        scores = mm(
            jnp.concatenate([k_hi, k_hi, k_lo], axis=1), jnp.concatenate([q_hi, q_lo, q_hi], axis=0)
        )
        key_at = lax.broadcasted_iota(jnp.int32, (CHUNK, CHUNK), 0)
        query_at = lax.broadcasted_iota(jnp.int32, (CHUNK, CHUNK), 1)
        s_hi, s_lo = split(jnp.where(key_at <= query_at, scores, 0.0))
        v_two, p_two = vt[b, n], pp[b, n]
        out = mm(
            jnp.concatenate([v_two, v_two, p_two, p_two], axis=1),
            jnp.concatenate([s_hi, s_lo, q_hi, q_lo], axis=0),
        )
        comb[b, n] = (out[:DH] + out[DH:]) * wrow[b, :, rows]
        for level in range(3):
            w_hi, w_lo = split(q_t * wrow[2 * (level + 1) + b, :, rows])
            wq[b, level * DH : (level + 1) * DH, rows] = w_hi
            wq[b, (3 + level) * DH : (4 + level) * DH, rows] = w_lo
        sc[b, n] = (cb[b, rows, :] * gain_ref[...]).T

    def local_chunks(b, low, high):
        @pl.loop(0, (high - low) // U_LOCAL)
        def _(i):
            for u in range(U_LOCAL):
                local_chunk(b, low + i * U_LOCAL + u)

    s1, s2, s4 = {}, {}, {}
    for b in range(2):
        loads["k", b].wait()
        loads["v", b].wait()
        load("qc", b)
        states(b)
        if b == 0:
            pl.semaphore_wait(barrier, len(peers))
        s1[b] = remote(st.at[b], b0.at[b], send_sem.at[0, b], recv_sem.at[0, b], to(mate))
        s1[b].start()

    def sum_pair(b):
        s1[b].wait_recv()
        mine = pl.ds(pl.multiple_of(core * half, half), half)
        pair[b] = st[b, mine, :] + b0[b, mine, :]
        s2[b] = [
            remote(pair.at[b], far_in.at[b, 0], send_sem.at[1, b], recv_sem.at[1, b], to(across)),
            remote(pair.at[b], far_in.at[b, 1], send_sem.at[2, b], recv_sem.at[2, b], to(far)),
            remote(pair.at[b], b12.at[b, core, 0], send_sem.at[3, b], recv_sem.at[3, b], to(near)),
        ]
        for copy in s2[b]:
            copy.start()

    def sum_quad(b):
        for copy in s2[b]:
            copy.wait_recv()
        b12[b, core, 1] = far_in[b, 0] + far_in[b, 1]
        s4[b] = remote(
            b12.at[b, core], b12.at[b, core], send_sem.at[4, b], recv_sem.at[4, b], to(mate)
        )
        s4[b].start()

    middle = n_chunks // 2
    sum_pair(0)
    loads["q", 0].wait()
    loads["c", 0].wait()
    local_chunks(0, 0, middle)
    sum_pair(1)
    local_chunks(0, middle, n_chunks)
    loads["q", 1].wait()
    loads["c", 1].wait()
    local_chunks(1, 0, middle)
    sum_quad(0)
    local_chunks(1, middle, n_chunks)

    def reads(b, sums):
        halves = [split(b0[b])]
        for level in range(2):
            halves.append(split(jnp.concatenate([b12[b, 0, level], b12[b, 1, level]], axis=0)))
        high = jnp.concatenate([h[0] for h in halves], axis=1)
        low = jnp.concatenate([h[1] for h in halves], axis=1)
        lb[b, :DH] = jnp.concatenate([high, high], axis=1)
        lb[b, DH:] = jnp.concatenate([low, low], axis=1)

        @pl.loop(0, n_chunks // U_READ)
        def _(i):
            for u in range(U_READ):
                n = i * U_READ + u
                out = mm(lb[b], wq[b, :, lanes(n)])
                mixed = comb[b, n] + (out[:DH] + out[DH:])
                comb[b, n] = mixed
                sums[pl.ds(n, 1), :] = jnp.sum(mixed * mixed, axis=0, keepdims=True)
                sums[pl.ds(n_chunks + n, 1), :] = jnp.sum(sc[b, n] * mixed, axis=0, keepdims=True)

    def arrived(buffer, count, sem):
        window = buffer.at[pl.ds(0, count)]
        pltpu.make_async_copy(window, window, sem).wait()

    z_order = sorted(range(1, n_z), key=lambda r: -min(r, n_z - r))
    x_stage = (x_in, x, [x_peers[r] for r in (1, 0, 2)], n_x - 1)
    z_stage = (z_in, z, [z_peers[r - 1] for r in z_order], n_z - 1)
    stages = ((z_stage, x_stage), (x_stage, z_stage))

    def send_sums(b, step):
        buffer, mine, others, _ = stages[b][step]
        for peer in others:
            remote(
                buffer.at[b, mine], buffer.at[b, mine], h_send.at[step, b], h_recv.at[step, b],
                along(peer),
            ).start()

    def receive_sums(b, step):
        buffer, _, _, count = stages[b][step]
        arrived(buffer.at[b], count, h_recv.at[step, b])
        return jnp.sum(buffer[b], axis=0)

    def pass_on(b):
        partial = receive_sums(b, 0)
        buffer, mine, _, _ = stages[b][1]
        buffer[b, mine] = partial
        send_sums(b, 1)

    def coefficients(b):
        whole = receive_sums(b, 1)
        width = n_x * n_z * DH
        inverse = lax.rsqrt(whole[:n_chunks] / width + EPS)
        coef[b, :n_chunks] = inverse
        coef[b, n_chunks:] = inverse * inverse * inverse * whole[n_chunks:] / width

    for b in range(2):
        s4[b].wait_recv()
        buffer, mine, _, _ = stages[b][0]
        reads(b, buffer.at[b, mine])
        send_sums(b, 0)
        if b == 0:
            sum_quad(1)
    pass_on(0)
    pass_on(1)

    def level_grads(b):
        gacc[...] = jnp.zeros_like(gacc)
        pieces = WIDE // CHUNK

        @pl.loop(0, tokens // WIDE)
        def _(n):
            parts = []
            for i in range(pieces):
                m = n * pieces + i
                grad = sc[b, m] * coef[b, pl.ds(m, 1), :] - comb[b, m] * coef[b, pl.ds(n_chunks + m, 1), :]
                parts.append(jnp.concatenate(split(grad), axis=0))
            rows = pl.ds(pl.multiple_of(n * WIDE, WIDE), WIDE)
            gacc[...] += mm_nt(wq[b, :, rows], jnp.concatenate(parts, axis=1))

        for level in range(3):
            top = slice(level * DH, (level + 1) * DH)
            bottom = slice((3 + level) * DH, (4 + level) * DH)
            grad = gacc[top, :DH] + (gacc[top, DH:] + gacc[bottom, :DH])
            if level == 0:
                gr0[b] = grad
            else:
                grh[b, 0, level - 1] = grad[:half]
                grh[b, 1, level - 1] = grad[half:]

    def attended(b):
        @pl.loop(0, n_chunks // U_ATT)
        def _(i):
            for u in range(U_ATT):
                n = i * U_ATT + u
                att_ref[b, lanes(n), :] = (comb[b, n] * coef[b, pl.ds(n, 1), :]).T * gain_ref[...]

    g1, g2, g4 = {}, {}, {}

    def send_mate(b):
        g1[b] = [
            remote(grh.at[b, other], t1.at[b], send_sem.at[5, b], recv_sem.at[5, b], to(mate)),
            remote(gr0.at[b], t0.at[b], send_sem.at[6, b], recv_sem.at[6, b], to(mate)),
        ]
        for copy in g1[b]:
            copy.start()

    def send_chips(b):
        g1[b][0].wait_recv()
        r12[b] = grh[b, core] + t1[b]
        g2[b] = [
            remote(r12.at[b, 1], r_in.at[b, 0], send_sem.at[7, b], recv_sem.at[7, b], to(across)),
            remote(r12.at[b, 1], r_in.at[b, 1], send_sem.at[8, b], recv_sem.at[8, b], to(far)),
            remote(r12.at[b, 0], r_in.at[b, 2], send_sem.at[9, b], recv_sem.at[9, b], to(near)),
        ]
        for copy in g2[b]:
            copy.start()

    def send_total(b):
        for copy in g2[b]:
            copy.wait_recv()
        total[b, core] = r_in[b, 0] + r_in[b, 1] + r_in[b, 2]
        g4[b] = remote(
            total.at[b, core], total.at[b, core], send_sem.at[10, b], recv_sem.at[10, b], to(mate)
        )
        g4[b].start()

    for b in range(2):
        coefficients(b)
        level_grads(b)
        send_mate(b)
        send_chips(b)
    attended(0)
    attended(1)
    send_total(0)
    send_total(1)
    for b in range(2):
        g1[b][1].wait_recv()
        g4[b].wait_recv()
        sg_ref[b, 0, :half] = total[b, 0] + t0[b, :half]
        sg_ref[b, 0, half:] = total[b, 1] + t0[b, half:]

    for b in range(2):
        for copy in (s1[b], s4[b], g4[b], *s2[b], *g1[b], *g2[b]):
            copy.wait_send()
        for step in range(2):
            buffer, _, _, count = stages[b][step]
            arrived(buffer.at[b], count, h_send.at[step, b])


def solution(mesh):
    n_z = mesh.shape["head"] // N_X

    def local(
        query_rows, key_rows, value_rows, cotangent, selector, level_table, span_length, norm_gain
    ):
        batch, tokens, _ = query_rows.shape
        n_chunks = tokens // CHUNK
        square = (DH, DH)
        half = (DH // 2, DH)
        whole = (batch, tokens, DH)
        scratch = [
            pltpu.VMEM((batch, 1, tokens), jnp.int32),
            pltpu.SMEM((4, 16), F32),
            pltpu.SMEM((1, batch), jnp.int32),
            pltpu.VMEM((1, DH), F32),
        ]
        scratch += [pltpu.VMEM(whole, F32) for _ in range(4)]
        scratch += [
            pltpu.VMEM(whole, BF16),
            pltpu.VMEM(whole, BF16),
            pltpu.VMEM((batch, n_chunks, 2 * DH, CHUNK), BF16),
            pltpu.VMEM((batch, n_chunks, 2 * DH, DH), BF16),
            pltpu.VMEM((4 * batch, 1, tokens), F32),
            pltpu.VMEM((batch, 6 * DH, tokens), BF16),
            pltpu.VMEM((batch, n_chunks, DH, CHUNK), F32),
            pltpu.VMEM((batch, n_chunks, DH, CHUNK), F32),
            pltpu.VMEM((6 * DH, 2 * DH), F32),
            pltpu.VMEM((batch, *square), F32),
            pltpu.VMEM((batch, *square), F32),
            pltpu.VMEM((batch, *half), F32),
            pltpu.VMEM((batch, 2, 2, *half), F32),
            pltpu.VMEM((batch, 2, *half), F32),
            pltpu.VMEM((batch, 2 * DH, 6 * DH), BF16),
            pltpu.VMEM((batch, N_X, 2 * n_chunks, CHUNK), F32),
            pltpu.VMEM((batch, n_z, 2 * n_chunks, CHUNK), F32),
            pltpu.VMEM((batch, 2 * n_chunks, CHUNK), F32),
            pltpu.VMEM((batch, *square), F32),
            pltpu.VMEM((batch, 2, 2, *half), F32),
            pltpu.VMEM((batch, *square), F32),
            pltpu.VMEM((batch, 2, *half), F32),
            pltpu.VMEM((batch, 2, *half), F32),
            pltpu.VMEM((batch, 3, *half), F32),
            pltpu.VMEM((batch, 2, *half), F32),
            pltpu.SemaphoreType.DMA((4, 2)),
            pltpu.SemaphoreType.DMA((4,)),
            pltpu.SemaphoreType.DMA((11, 2)),
            pltpu.SemaphoreType.DMA((11, 2)),
            pltpu.SemaphoreType.DMA((2, 2)),
            pltpu.SemaphoreType.DMA((2, 2)),
        ]
        hbm = pl.BlockSpec(memory_space=pltpu.HBM)
        vmem = pl.BlockSpec(memory_space=pltpu.VMEM)
        return pl.pallas_call(
            functools.partial(kernel, N_X, n_z, tokens),
            out_shape=(
                jax.ShapeDtypeStruct(whole, F32),
                jax.ShapeDtypeStruct((batch, 1, DH, DH), F32),
            ),
            in_specs=[hbm] * 8,
            out_specs=(vmem, vmem),
            scratch_shapes=scratch,
            compiler_params=pltpu.CompilerParams(
                collective_id=0, has_side_effects=True, vmem_limit_bytes=50 * 2**20
            ),
            cost_estimate=pl.CostEstimate(
                flops=2 * 10**10, bytes_accessed=12 * 2**20, transcendentals=0
            ),
        )(
            query_rows, key_rows, value_rows, cotangent,
            *(
                pltpu.with_memory_space_constraint(small, pltpu.HBM)
                for small in (selector, level_table.T, span_length.T, norm_gain.reshape(1, DH))
            ),
        )

    return jax.shard_map(
        local,
        mesh=mesh,
        in_specs=(
            P(None, "seq", "head"),
            P(None, "seq", "head"),
            P(None, "seq", "head"),
            P(None, "seq", "head"),
            P(None, "head", "seq"),
            P(),
            P(None, "seq"),
            P("head"),
        ),
        out_specs=(P(None, "seq", "head"), P(None, "seq", None, "head")),
        check_vma=False,
    )
```
